32 devices in a mesh: blk: 8 (over z, x), grp: 4 (over y, core).
Axes of the slice: x: 2, y: 2, z: 4, core: 2. Of those that a mesh axis runs over, the one named last changes fastest.
Arguments:
- image_student: bfloat16 [8, 4, 256, 768], P('blk', 'grp'), may hold values from -6 to 6
- image_teacher: bfloat16 [8, 4, 256, 1152], P('blk', 'grp'), may hold values from -6 to 6
- text_student: bfloat16 [8, 4, 256, 768], P('blk', 'grp'), may hold values from -6 to 6
- text_teacher: bfloat16 [8, 4, 256, 1152], P('blk', 'grp'), may hold values from -6 to 6
- pair_ids: int32 [8, 4, 256], P('blk', 'grp'), may hold values from 0 to 511
Outputs:
- image_grad: float32 [8, 4, 256, 768], P('blk', 'grp')
- text_grad: float32 [8, 4, 256, 768], P('blk', 'grp')
- bias_grad: float32 [], replicated
The draws below stay inside these ranges and needn't reach their ends.
All inputs are finite; a program needn't handle non-finite values.
Results may differ from the reference program's by a relative error of at most 0.0021.
Values may be sent and summed in bfloat16 or wider, within the bound.
A program may use at most 64 MiB of HBM per device.

```python
import math
import jax
import jax.numpy as jnp
from jax import lax

DS = 768
DT = 1152
P_SIZE = 256
WINDOW = 4
NB = 8
NG = 4
N_BLK = 8
N_GRP = 4


def touch_ends(values, rng, smallest, high):
    longest = values.shape.index(max(values.shape))
    spots = []
    for shift in (0, 1):
        where = [jax.random.randint(jax.random.fold_in(rng, axis), (), 0, length) for axis, length in enumerate(values.shape)]
        where[longest] = (where[longest] + shift) % values.shape[longest]
        spots.append(tuple(where))
    return values.at[spots[0]].set(smallest).at[spots[1]].set(high)


def block_scale(own_key, extent, split, least, high):
    loudness, own = 1.0, jax.random.fold_in(own_key, 6)
    for axis_at, blocks in split:
        steps = jnp.exp(jax.random.uniform(jax.random.fold_in(own, axis_at), (blocks,), jnp.float32, least / len(split), high / len(split)))
        loudness = loudness * jnp.repeat(steps, extent[axis_at] // blocks).reshape([-1 if axis == axis_at else 1 for axis in range(len(extent))])
    return loudness


def bell_draw(stream_key, extent, spread, most, split=(), dtype=jnp.bfloat16):
    factor_of = block_scale(stream_key, extent, split, -0.22, 0.18) if split else 1.0
    entries = jax.random.normal(stream_key, extent, jnp.float32) * spread * factor_of
    return jnp.minimum(jnp.maximum(entries, -most), most).astype(dtype)


def setup_inputs(seed: int = 0) -> dict:
    streams_of = jax.random.split(jax.random.key(seed), 6)
    image_student = bell_draw(streams_of[0], (NB, NG, P_SIZE, DS), 1.0, 6.0, ((0, 8), (1, 4)))
    image_teacher = bell_draw(streams_of[1], (NB, NG, P_SIZE, DT), 1.0, 6.0, ((0, 8), (1, 4)))
    text_student = bell_draw(streams_of[2], (NB, NG, P_SIZE, DS), 1.0, 6.0, ((0, 8), (1, 4)))
    text_teacher = bell_draw(streams_of[3], (NB, NG, P_SIZE, DT), 1.0, 6.0, ((0, 8), (1, 4)))
    pair_ids = touch_ends(jax.random.randint(streams_of[4], (NB, NG, P_SIZE), 0, 2 * P_SIZE), jax.random.fold_in(streams_of[4], 1), 0, (2 * P_SIZE) - 1).astype(jnp.int32)
    return dict(image_student=image_student, image_teacher=image_teacher, text_student=text_student, text_teacher=text_teacher, pair_ids=pair_ids)


def reference(image_student, image_teacher, text_student, text_teacher, pair_ids):
    scale_s = 2.0 / math.sqrt(DS)
    scale_t = 2.0 / math.sqrt(DT)
    img_stu = image_student.astype(jnp.float32)
    img_tea = image_teacher.astype(jnp.float32)
    image_grad = jnp.zeros(img_stu.shape, jnp.float32)
    text_grad = jnp.zeros(img_stu.shape, jnp.float32)
    total = jnp.float32(0.0)
    for offset in range(WINDOW):
        txt_stu = jnp.roll(text_student, offset, axis=0).astype(jnp.float32)
        txt_tea = jnp.roll(text_teacher, offset, axis=0).astype(jnp.float32)
        txt_ids = jnp.roll(pair_ids, offset, axis=0)
        scores = jnp.einsum('bgpd,bgqd->bgpq', img_stu, txt_stu) * scale_s - 1.0
        teacher = jnp.einsum('bgpd,bgqd->bgpq', img_tea, txt_tea) * scale_t - 1.0
        match = (pair_ids[:, :, :, None] == txt_ids[:, :, None, :]).astype(jnp.float32)
        weights = jax.nn.sigmoid(scores) - 0.5 * jax.nn.sigmoid(teacher) - 0.5 * match
        total = total + jnp.sum(weights)
        rounded = lax.optimization_barrier(weights.astype(jnp.bfloat16)).astype(jnp.float32)
        image_grad = image_grad + jnp.einsum('bgpq,bgqd->bgpd', rounded, txt_stu) * scale_s
        partial_txt = jnp.einsum('bgpq,bgpd->bgqd', rounded, img_stu) * scale_s
        text_grad = text_grad + jnp.roll(partial_txt, -offset, axis=0)
    count = float(N_BLK * N_GRP * WINDOW * P_SIZE * P_SIZE)
    return (image_grad, text_grad, total / count)
```

```python
import functools
import math

import jax
import jax.numpy as jnp
from jax import lax
from jax.experimental import pallas as pl
from jax.experimental.pallas import tpu as pltpu
from jax.sharding import PartitionSpec as P

MESH = pl.DeviceIdType.MESH
WINDOW = 4
F_CHUNKS = 4
N_CHUNKS = 4
OUT_CHUNKS = 4


def dot_nt(a, b):
    return lax.dot_general(a, b, (((1,), (1,)), ((), ())), preferred_element_type=jnp.float32)


def dot_tn(a, b):
    return lax.dot_general(a, b, (((0,), (0,)), ((), ())), preferred_element_type=jnp.float32)


def dot_nn(a, b):
    return jnp.dot(a, b, preferred_element_type=jnp.float32)


def fold(w):
    w = jnp.sum(w.reshape(w.shape[0] // 8, 8, w.shape[1]), axis=0)
    out = w[:, 0:128]
    for at in range(128, w.shape[1], 128):
        out = out + w[:, at : at + 128]
    return out


def kernel(
    n_blk,
    n_grp,
    ds,
    inv_count,
    img_stu,
    img_tea,
    txt_stu,
    txt_tea,
    ids,
    out_img,
    out_txt,
    out_bias,
    far,
    near,
    own_ids,
    far_in,
    near_in,
    far_ids_in,
    near_ids_in,
    acc_far,
    acc_near,
    acc_pn,
    pf_out,
    pn_out,
    pf_in,
    pn_in,
    total,
    stage1_own,
    stage1,
    stage2_own,
    stage2,
    local_sem,
    far_send,
    far_recv,
    near_send,
    near_recv,
    ids_send,
    ids_recv,
    pf_send,
    pf_recv,
    pn_send,
    pn_recv,
    s1_send,
    s1_recv,
    s2_send,
    s2_recv,
):
    b = lax.axis_index("blk")
    g = lax.axis_index("grp")
    size = far.shape[0]
    dt = far.shape[1] - ds
    role = lax.rem(g, 2)
    step = 1 - 2 * role
    far_to = lax.rem(b + 2 * step + 2 * n_blk, n_blk)
    far_from = lax.rem(b - 2 * step + 2 * n_blk, n_blk)
    near_to = lax.rem(b - step + n_blk, n_blk)
    near_from = lax.rem(b + step + n_blk, n_blk)

    def at_blk(i):
        return {"blk": i, "grp": g}

    def loads(f_stu, f_tea, n_stu, n_tea):
        return [
            pltpu.make_async_copy(f_stu, far.at[:, pl.ds(0, ds)], local_sem.at[0]),
            pltpu.make_async_copy(f_tea, far.at[:, pl.ds(ds, dt)], local_sem.at[1]),
            pltpu.make_async_copy(n_stu, near.at[:, pl.ds(0, ds)], local_sem.at[2]),
            pltpu.make_async_copy(n_tea, near.at[:, pl.ds(ds, dt)], local_sem.at[3]),
        ]

    @pl.when(role == 0)
    def _():
        for c in loads(txt_stu, txt_tea, img_stu, img_tea):
            c.start()

    @pl.when(role == 1)
    def _():
        for c in loads(img_stu, img_tea, txt_stu, txt_tea):
            c.start()

    ids_load = pltpu.make_async_copy(ids, own_ids, local_sem.at[4])
    ids_load.start()

    barrier = pltpu.get_barrier_semaphore()
    for k in range(1, n_blk):
        pl.semaphore_signal(
            barrier, inc=1, device_id=at_blk(lax.rem(b + k, n_blk)), device_id_type=MESH
        )
    for k in range(1, n_grp):
        pl.semaphore_signal(
            barrier,
            inc=1,
            device_id={"blk": b, "grp": lax.rem(g + k, n_grp)},
            device_id_type=MESH,
        )
    for c in loads(txt_stu, txt_tea, img_stu, img_tea):
        c.wait()
    ids_load.wait()
    pl.semaphore_wait(barrier, n_blk - 1 + n_grp - 1)

    def remote(src, dst, send, recv, to):
        return pltpu.make_async_remote_copy(
            src_ref=src, dst_ref=dst, send_sem=send, recv_sem=recv,
            device_id=to, device_id_type=MESH,
        )

    fr = size // F_CHUNKS
    nr = size // N_CHUNKS
    ids_f = remote(own_ids, far_ids_in, ids_send.at[0], ids_recv.at[0], at_blk(far_to))
    ids_n = remote(own_ids, near_ids_in, ids_send.at[1], ids_recv.at[1], at_blk(near_to))
    ids_n.start()
    ids_f.start()
    near_copies = [
        remote(
            near.at[pl.ds(j * nr, nr)], near_in.at[pl.ds(j * nr, nr)],
            near_send.at[j], near_recv.at[j], at_blk(near_to),
        )
        for j in range(N_CHUNKS)
    ]
    far_copies = [
        remote(
            far.at[pl.ds(i * fr, fr)], far_in.at[pl.ds(i * fr, fr)],
            far_send.at[i], far_recv.at[i], at_blk(far_to),
        )
        for i in range(F_CHUNKS)
    ]
    for c in near_copies:
        c.start()
    for c in far_copies:
        c.start()

    scale_s = 2.0 / math.sqrt(ds)
    scale_t = 2.0 / math.sqrt(dt)

    def as_column(row):
        return jnp.transpose(jnp.broadcast_to(row, (128, row.shape[1])))[:, 0:1]

    def weigh(f, n, f_id, n_id):
        s = dot_nt(f[:, :ds], n[:, :ds]) * (0.5 * scale_s) - 0.5
        q = dot_nt(f[:, ds:], n[:, ds:]) * (0.5 * scale_t) - 0.5
        shift = jnp.where(f_id == n_id, -0.25, 0.25)
        return 0.5 * jnp.tanh(s) - 0.25 * jnp.tanh(q) + shift

    own_row = own_ids[...]
    own_col = as_column(own_row)

    w = weigh(far[...], near[...], own_col, own_row)
    total[...] = fold(w)
    wb = w.astype(jnp.bfloat16)
    acc_far[...] = dot_nn(wb, near[:, :ds])
    acc_near[...] = dot_tn(wb, far[:, :ds])

    ids_n.wait_recv()
    near_row = near_ids_in[...]
    for j in range(N_CHUNKS):
        near_copies[j].wait_recv()
        rows = pl.ds(j * nr, nr)
        w = weigh(near_in[rows, :], far[...], as_column(near_row)[j * nr : (j + 1) * nr], own_row)
        total[...] += fold(w)
        wb = w.astype(jnp.bfloat16)
        acc_far[...] += dot_tn(wb, near_in[rows, pl.ds(0, ds)])
        acc_pn[rows, :] = dot_nn(wb, far[:, :ds])

    ids_f.wait_recv()
    far_col = as_column(far_ids_in[...])
    pf_copies = []
    for i in range(F_CHUNKS):
        far_copies[i].wait_recv()
        rows = pl.ds(i * fr, fr)
        f = far_in[rows, :]
        f_id = far_col[i * fr : (i + 1) * fr]
        w1 = weigh(f, near[...], f_id, own_row)
        w2 = weigh(f, near_in[...], f_id, near_row)
        total[...] += fold(w1) + fold(w2)
        w1 = w1.astype(jnp.bfloat16)
        w2 = w2.astype(jnp.bfloat16)
        back = dot_nn(w1, near[:, :ds]) + dot_nn(w2, near_in[:, :ds])
        pf_out[rows, :] = (back * scale_s).astype(jnp.bfloat16)
        c = remote(
            pf_out.at[rows], pf_in.at[rows], pf_send.at[i], pf_recv.at[i], at_blk(far_from)
        )
        c.start()
        pf_copies.append(c)
        acc_near[...] += dot_tn(w1, f[:, :ds])
        acc_pn[...] += dot_tn(w2, f[:, :ds])

    stage1_own[...] = total[...]
    stage1[pl.ds(b, 1)] = total[...][None]
    s1 = []
    for k in range(1, n_blk):
        c = remote(
            stage1_own, stage1.at[b], s1_send.at[k - 1], s1_recv.at[k - 1],
            at_blk(lax.rem(b + k, n_blk)),
        )
        c.start()
        s1.append(c)

    pr = size // OUT_CHUNKS
    pn_copies = []
    for j in range(OUT_CHUNKS):
        rows = pl.ds(j * pr, pr)
        pn_out[rows, :] = (acc_pn[rows, :] * scale_s).astype(jnp.bfloat16)
        c = remote(
            pn_out.at[rows], pn_in.at[rows], pn_send.at[j], pn_recv.at[j], at_blk(near_from)
        )
        c.start()
        pn_copies.append(c)

    for c in s1:
        c.wait_recv()
    part = stage1[0]
    for k in range(1, n_blk):
        part = part + stage1[k]
    stage2_own[...] = part
    stage2[pl.ds(g, 1)] = part[None]
    s2 = []
    for k in range(1, n_grp):
        c = remote(
            stage2_own, stage2.at[g], s2_send.at[k - 1], s2_recv.at[k - 1],
            {"blk": b, "grp": lax.rem(g + k, n_grp)},
        )
        c.start()
        s2.append(c)

    def finish(copies, acc, arrived, rows_each, out_a, out_b):
        for i, c in enumerate(copies):
            c.wait_recv()
            rows = pl.ds(i * rows_each, rows_each)
            value = acc[rows, :] * scale_s + arrived[rows, :].astype(jnp.float32)

            @pl.when(role == 0)
            def _():
                out_a[rows, :] = value

            @pl.when(role == 1)
            def _():
                out_b[rows, :] = value

    finish(pf_copies, acc_far, pf_in, fr, out_txt, out_img)
    finish(pn_copies, acc_near, pn_in, pr, out_img, out_txt)

    for c in s2:
        c.wait_recv()
    whole = stage2[0]
    for k in range(1, n_grp):
        whole = whole + stage2[k]
    out_bias[0, 0] = jnp.sum(whole) * inv_count

    for c in [ids_f, ids_n] + near_copies + far_copies + pf_copies + pn_copies + s1 + s2:
        c.wait_send()


def solution(mesh):
    n_blk, n_grp = mesh.shape["blk"], mesh.shape["grp"]

    def body(image_student, image_teacher, text_student, text_teacher, pair_ids):
        size, ds = image_student.shape[2:]
        dt = image_teacher.shape[3]
        bf, f32 = jnp.bfloat16, jnp.float32
        dma = lambda k: pltpu.SemaphoreType.DMA((max(k, 1),))
        count = float(n_blk * n_grp * WINDOW * size * size)
        img, txt, bias = pl.pallas_call(
            functools.partial(kernel, n_blk, n_grp, ds, 1.0 / count),
            out_shape=(
                jax.ShapeDtypeStruct((size, ds), f32),
                jax.ShapeDtypeStruct((size, ds), f32),
                jax.ShapeDtypeStruct((1, 1), f32),
            ),
            in_specs=[pl.BlockSpec(memory_space=pl.ANY)] * 5,
            out_specs=(
                pl.BlockSpec(memory_space=pltpu.VMEM),
                pl.BlockSpec(memory_space=pltpu.VMEM),
                pl.BlockSpec(memory_space=pltpu.SMEM),
            ),
            scratch_shapes=[
                pltpu.VMEM((size, ds + dt), bf),
                pltpu.VMEM((size, ds + dt), bf),
                pltpu.VMEM((1, size), jnp.int32),
                pltpu.VMEM((size, ds + dt), bf),
                pltpu.VMEM((size, ds + dt), bf),
                pltpu.VMEM((1, size), jnp.int32),
                pltpu.VMEM((1, size), jnp.int32),
                pltpu.VMEM((size, ds), f32),
                pltpu.VMEM((size, ds), f32),
                pltpu.VMEM((size, ds), f32),
                pltpu.VMEM((size, ds), bf),
                pltpu.VMEM((size, ds), bf),
                pltpu.VMEM((size, ds), bf),
                pltpu.VMEM((size, ds), bf),
                pltpu.VMEM((8, 128), f32),
                pltpu.VMEM((8, 128), f32),
                pltpu.VMEM((n_blk, 8, 128), f32),
                pltpu.VMEM((8, 128), f32),
                pltpu.VMEM((n_grp, 8, 128), f32),
                dma(5),
                dma(F_CHUNKS),
                dma(F_CHUNKS),
                dma(N_CHUNKS),
                dma(N_CHUNKS),
                dma(2),
                dma(2),
                dma(F_CHUNKS),
                dma(F_CHUNKS),
                dma(OUT_CHUNKS),
                dma(OUT_CHUNKS),
                dma(n_blk - 1),
                dma(n_blk - 1),
                dma(n_grp - 1),
                dma(n_grp - 1),
            ],
            compiler_params=pltpu.CompilerParams(
                collective_id=0, has_side_effects=True, vmem_limit_bytes=40 * 1024 * 1024
            ),
        )(
            image_student[0, 0],
            image_teacher[0, 0],
            text_student[0, 0],
            text_teacher[0, 0],
            pair_ids[0],
        )
        return img[None, None], txt[None, None], bias[0, 0]

    return jax.shard_map(
        body,
        mesh=mesh,
        in_specs=(
            P("blk", "grp", None, None),
            P("blk", "grp", None, None),
            P("blk", "grp", None, None),
            P("blk", "grp", None, None),
            P("blk", "grp", None),
        ),
        out_specs=(P("blk", "grp", None, None), P("blk", "grp", None, None), P()),
        check_vma=False,
    )
```

```python
import functools
import math

import jax
import jax.numpy as jnp
from jax import lax
from jax.experimental import pallas as pl
from jax.experimental.pallas import tpu as pltpu
from jax.sharding import PartitionSpec as P

MESH = pl.DeviceIdType.MESH
WINDOW = 4
F_CHUNKS = 4
N_CHUNKS = 4
OUT_CHUNKS = 4


def dot_nt(a, b):
    return lax.dot_general(a, b, (((1,), (1,)), ((), ())), preferred_element_type=jnp.float32)


def dot_tn(a, b):
    return lax.dot_general(a, b, (((0,), (0,)), ((), ())), preferred_element_type=jnp.float32)


def dot_nn(a, b):
    return jnp.dot(a, b, preferred_element_type=jnp.float32)


def fold(w):
    w = jnp.sum(w.reshape(w.shape[0] // 8, 8, w.shape[1]), axis=0)
    out = w[:, 0:128]
    for at in range(128, w.shape[1], 128):
        out = out + w[:, at : at + 128]
    return out


def kernel(
    n_blk,
    n_grp,
    ds,
    inv_count,
    img_stu,
    img_tea,
    txt_stu,
    txt_tea,
    ids,
    out_img,
    out_txt,
    out_bias,
    far,
    near,
    own_ids,
    far_in,
    near_in,
    far_ids_in,
    near_ids_in,
    acc_far,
    acc_near,
    acc_pn,
    pf_out,
    pn_out,
    pf_in,
    pn_in,
    total,
    stage1_own,
    stage1,
    stage2_own,
    stage2,
    local_sem,
    far_send,
    far_recv,
    near_send,
    near_recv,
    ids_send,
    ids_recv,
    pf_send,
    pf_recv,
    pn_send,
    pn_recv,
    s1_send,
    s1_recv,
    s2_send,
    s2_recv,
):
    b = lax.axis_index("blk")
    g = lax.axis_index("grp")
    size = far.shape[0]
    dt = far.shape[1] - ds
    role = lax.rem(g, 2)
    step = 1 - 2 * role
    far_to = lax.rem(b + 2 * step + 2 * n_blk, n_blk)
    far_from = lax.rem(b - 2 * step + 2 * n_blk, n_blk)
    near_to = lax.rem(b - step + n_blk, n_blk)
    near_from = lax.rem(b + step + n_blk, n_blk)

    def at_blk(i):
        return {"blk": i, "grp": g}

    def loads(f_stu, f_tea, n_stu, n_tea):
        return [
            pltpu.make_async_copy(f_stu, far.at[:, pl.ds(0, ds)], local_sem.at[0]),
            pltpu.make_async_copy(f_tea, far.at[:, pl.ds(ds, dt)], local_sem.at[1]),
            pltpu.make_async_copy(n_stu, near.at[:, pl.ds(0, ds)], local_sem.at[2]),
            pltpu.make_async_copy(n_tea, near.at[:, pl.ds(ds, dt)], local_sem.at[3]),
        ]

    @pl.when(role == 0)
    def _():
        for c in loads(txt_stu, txt_tea, img_stu, img_tea):
            c.start()

    @pl.when(role == 1)
    def _():
        for c in loads(img_stu, img_tea, txt_stu, txt_tea):
            c.start()

    ids_load = pltpu.make_async_copy(ids, own_ids, local_sem.at[4])
    ids_load.start()

    barrier = pltpu.get_barrier_semaphore()
    for k in range(1, n_blk):
        pl.semaphore_signal(
            barrier, inc=1, device_id=at_blk(lax.rem(b + k, n_blk)), device_id_type=MESH
        )
    for k in range(1, n_grp):
        pl.semaphore_signal(
            barrier,
            inc=1,
            device_id={"blk": b, "grp": lax.rem(g + k, n_grp)},
            device_id_type=MESH,
        )
    for c in loads(txt_stu, txt_tea, img_stu, img_tea):
        c.wait()
    ids_load.wait()
    pl.semaphore_wait(barrier, n_blk - 1 + n_grp - 1)

    def remote(src, dst, send, recv, to):
        return pltpu.make_async_remote_copy(
            src_ref=src, dst_ref=dst, send_sem=send, recv_sem=recv,
            device_id=to, device_id_type=MESH,
        )

    fr = size // F_CHUNKS
    nr = size // N_CHUNKS
    ids_f = remote(own_ids, far_ids_in, ids_send.at[0], ids_recv.at[0], at_blk(far_to))
    ids_n = remote(own_ids, near_ids_in, ids_send.at[1], ids_recv.at[1], at_blk(near_to))
    ids_n.start()
    ids_f.start()
    near_copies = [
        remote(
            near.at[pl.ds(j * nr, nr)], near_in.at[pl.ds(j * nr, nr)],
            near_send.at[j], near_recv.at[j], at_blk(near_to),
        )
        for j in range(N_CHUNKS)
    ]
    far_copies = [
        remote(
            far.at[pl.ds(i * fr, fr)], far_in.at[pl.ds(i * fr, fr)],
            far_send.at[i], far_recv.at[i], at_blk(far_to),
        )
        for i in range(F_CHUNKS)
    ]
    for c in near_copies:
        c.start()
    for c in far_copies:
        c.start()

    scale_s = 2.0 / math.sqrt(ds)
    scale_t = 2.0 / math.sqrt(dt)

    def as_column(row):
        return jnp.transpose(jnp.broadcast_to(row, (128, row.shape[1])))[:, 0:1]

    def weigh(f, n, f_id, n_id):
        s = dot_nt(f[:, :ds], n[:, :ds]) * (0.5 * scale_s) - 0.5
        q = dot_nt(f[:, ds:], n[:, ds:]) * (0.5 * scale_t) - 0.5
        shift = jnp.where(f_id == n_id, -0.25, 0.25)
        return 0.5 * jnp.tanh(s) - 0.25 * jnp.tanh(q) + shift

    own_row = own_ids[...]
    own_col = as_column(own_row)

    w = weigh(far[...], near[...], own_col, own_row)
    total[...] = fold(w)
    wb = w.astype(jnp.bfloat16)
    acc_far[...] = dot_nn(wb, near[:, :ds])
    acc_near[...] = dot_tn(wb, far[:, :ds])

    ids_n.wait_recv()
    near_row = near_ids_in[...]
    for j in range(N_CHUNKS):
        near_copies[j].wait_recv()
        rows = pl.ds(j * nr, nr)
        w = weigh(near_in[rows, :], far[...], as_column(near_row)[j * nr : (j + 1) * nr], own_row)
        total[...] += fold(w)
        wb = w.astype(jnp.bfloat16)
        acc_far[...] += dot_tn(wb, near_in[rows, pl.ds(0, ds)])
        acc_pn[rows, :] = dot_nn(wb, far[:, :ds])

    ids_f.wait_recv()
    far_col = as_column(far_ids_in[...])
    pf_copies = []
    for i in range(F_CHUNKS):
        far_copies[i].wait_recv()
        rows = pl.ds(i * fr, fr)
        f = far_in[rows, :]
        f_id = far_col[i * fr : (i + 1) * fr]
        w1 = weigh(f, near[...], f_id, own_row)
        w2 = weigh(f, near_in[...], f_id, near_row)
        total[...] += fold(w1) + fold(w2)
        w1 = w1.astype(jnp.bfloat16)
        w2 = w2.astype(jnp.bfloat16)
        back = dot_nn(w1, near[:, :ds]) + dot_nn(w2, near_in[:, :ds])
        pf_out[rows, :] = (back * scale_s).astype(jnp.bfloat16)
        c = remote(
            pf_out.at[rows], pf_in.at[rows], pf_send.at[i], pf_recv.at[i], at_blk(far_from)
        )
        c.start()
        pf_copies.append(c)
        acc_near[...] += dot_tn(w1, f[:, :ds])
        acc_pn[...] += dot_tn(w2, f[:, :ds])

    stage1_own[...] = total[...]
    stage1[pl.ds(b, 1)] = total[...][None]
    s1 = []
    for k in range(1, n_blk):
        c = remote(
            stage1_own, stage1.at[b], s1_send.at[k - 1], s1_recv.at[k - 1],
            at_blk(lax.rem(b + k, n_blk)),
        )
        c.start()
        s1.append(c)

    pr = size // OUT_CHUNKS
    pn_copies = []
    for j in range(OUT_CHUNKS):
        rows = pl.ds(j * pr, pr)
        pn_out[rows, :] = (acc_pn[rows, :] * scale_s).astype(jnp.bfloat16)
        c = remote(
            pn_out.at[rows], pn_in.at[rows], pn_send.at[j], pn_recv.at[j], at_blk(near_from)
        )
        c.start()
        pn_copies.append(c)

    for c in s1:
        c.wait_recv()
    part = stage1[0]
    for k in range(1, n_blk):
        part = part + stage1[k]
    stage2_own[...] = part
    stage2[pl.ds(g, 1)] = part[None]
    s2 = []
    for k in range(1, n_grp):
        c = remote(
            stage2_own, stage2.at[g], s2_send.at[k - 1], s2_recv.at[k - 1],
            {"blk": b, "grp": lax.rem(g + k, n_grp)},
        )
        c.start()
        s2.append(c)

    def finish(copies, acc, arrived, rows_each, out_a, out_b):
        for i, c in enumerate(copies):
            c.wait_recv()
            rows = pl.ds(i * rows_each, rows_each)
            value = acc[rows, :] * scale_s + arrived[rows, :].astype(jnp.float32)

            @pl.when(role == 0)
            def _():
                out_a[rows, :] = value

            @pl.when(role == 1)
            def _():
                out_b[rows, :] = value

    finish(pf_copies, acc_far, pf_in, fr, out_txt, out_img)
    finish(pn_copies, acc_near, pn_in, pr, out_img, out_txt)

    for c in s2:
        c.wait_recv()
    whole = stage2[0]
    for k in range(1, n_grp):
        whole = whole + stage2[k]
    out_bias[0, 0] = jnp.sum(whole) * inv_count

    for c in [ids_f, ids_n] + near_copies + far_copies + pf_copies + pn_copies + s1 + s2:
        c.wait_send()


def solution(mesh):
    n_blk, n_grp = mesh.shape["blk"], mesh.shape["grp"]

    def body(image_student, image_teacher, text_student, text_teacher, pair_ids):
        size, ds = image_student.shape[2:]
        dt = image_teacher.shape[3]
        bf, f32 = jnp.bfloat16, jnp.float32
        dma = lambda k: pltpu.SemaphoreType.DMA((max(k, 1),))
        count = float(n_blk * n_grp * WINDOW * size * size)
        img, txt, bias = pl.pallas_call(
            functools.partial(kernel, n_blk, n_grp, ds, 1.0 / count),
            out_shape=(
                jax.ShapeDtypeStruct((size, ds), f32),
                jax.ShapeDtypeStruct((size, ds), f32),
                jax.ShapeDtypeStruct((1, 1), f32),
            ),
            in_specs=[pl.BlockSpec(memory_space=pl.ANY)] * 5,
            out_specs=(
                pl.BlockSpec(memory_space=pltpu.VMEM),
                pl.BlockSpec(memory_space=pltpu.VMEM),
                pl.BlockSpec(memory_space=pltpu.SMEM),
            ),
            scratch_shapes=[
                pltpu.VMEM((size, ds + dt), bf),
                pltpu.VMEM((size, ds + dt), bf),
                pltpu.VMEM((1, size), jnp.int32),
                pltpu.VMEM((size, ds + dt), bf),
                pltpu.VMEM((size, ds + dt), bf),
                pltpu.VMEM((1, size), jnp.int32),
                pltpu.VMEM((1, size), jnp.int32),
                pltpu.VMEM((size, ds), f32),
                pltpu.VMEM((size, ds), f32),
                pltpu.VMEM((size, ds), f32),
                pltpu.VMEM((size, ds), bf),
                pltpu.VMEM((size, ds), bf),
                pltpu.VMEM((size, ds), bf),
                pltpu.VMEM((size, ds), bf),
                pltpu.VMEM((8, 128), f32),
                pltpu.VMEM((8, 128), f32),
                pltpu.VMEM((n_blk, 8, 128), f32),
                pltpu.VMEM((8, 128), f32),
                pltpu.VMEM((n_grp, 8, 128), f32),
                dma(5),
                dma(F_CHUNKS),
                dma(F_CHUNKS),
                dma(N_CHUNKS),
                dma(N_CHUNKS),
                dma(2),
                dma(2),
                dma(F_CHUNKS),
                dma(F_CHUNKS),
                dma(OUT_CHUNKS),
                dma(OUT_CHUNKS),
                dma(n_blk - 1),
                dma(n_blk - 1),
                dma(n_grp - 1),
                dma(n_grp - 1),
            ],
            compiler_params=pltpu.CompilerParams(
                collective_id=0, has_side_effects=True, vmem_limit_bytes=62 * 1024 * 1024
            ),
        )(
            image_student[0, 0],
            image_teacher[0, 0],
            text_student[0, 0],
            text_teacher[0, 0],
            pair_ids[0],
        )
        return img[None, None], txt[None, None], bias[0, 0]

    return jax.shard_map(
        body,
        mesh=mesh,
        in_specs=(
            P("blk", "grp", None, None),
            P("blk", "grp", None, None),
            P("blk", "grp", None, None),
            P("blk", "grp", None, None),
            P("blk", "grp", None),
        ),
        out_specs=(P("blk", "grp", None, None), P("blk", "grp", None, None), P()),
        check_vma=False,
    )
```

```python
import functools
import math

import jax
import jax.numpy as jnp
from jax import lax
from jax.experimental import pallas as pl
from jax.experimental.pallas import tpu as pltpu
from jax.sharding import PartitionSpec as P

MESH = pl.DeviceIdType.MESH
WINDOW = 4
F_CHUNKS = 4
N_CHUNKS = 4
OUT_CHUNKS = 4


def dot_nt(a, b):
    return lax.dot_general(a, b, (((1,), (1,)), ((), ())), preferred_element_type=jnp.float32)


def dot_tn(a, b):
    return lax.dot_general(a, b, (((0,), (0,)), ((), ())), preferred_element_type=jnp.float32)


def dot_nn(a, b):
    return jnp.dot(a, b, preferred_element_type=jnp.float32)


def fold(w):
    w = jnp.sum(w.reshape(w.shape[0] // 8, 8, w.shape[1]), axis=0)
    out = w[:, 0:128]
    for at in range(128, w.shape[1], 128):
        out = out + w[:, at : at + 128]
    return out


def kernel(
    n_blk,
    n_grp,
    ds,
    inv_count,
    img_stu,
    img_tea,
    txt_stu,
    txt_tea,
    ids,
    out_img,
    out_txt,
    out_bias,
    far,
    near,
    own_ids,
    far_in,
    near_in,
    far_ids_in,
    near_ids_in,
    acc_far,
    acc_near,
    acc_pn,
    pf_out,
    pn_out,
    pf_in,
    pn_in,
    total,
    stage1_own,
    stage1,
    stage2_own,
    stage2,
    local_sem,
    far_send,
    far_recv,
    near_send,
    near_recv,
    ids_send,
    ids_recv,
    pf_send,
    pf_recv,
    pn_send,
    pn_recv,
    s1_send,
    s1_recv,
    s2_send,
    s2_recv,
    out_sem,
):
    b = lax.axis_index("blk")
    g = lax.axis_index("grp")
    size = far.shape[0]
    dt = far.shape[1] - ds
    role = lax.rem(g, 2)
    step = 1 - 2 * role
    far_to = lax.rem(b + 2 * step + 2 * n_blk, n_blk)
    far_from = lax.rem(b - 2 * step + 2 * n_blk, n_blk)
    near_to = lax.rem(b - step + n_blk, n_blk)
    near_from = lax.rem(b + step + n_blk, n_blk)

    def at_blk(i):
        return {"blk": i, "grp": g}

    def loads(f_stu, f_tea, n_stu, n_tea):
        return [
            pltpu.make_async_copy(f_stu, far.at[:, pl.ds(0, ds)], local_sem.at[0]),
            pltpu.make_async_copy(f_tea, far.at[:, pl.ds(ds, dt)], local_sem.at[1]),
            pltpu.make_async_copy(n_stu, near.at[:, pl.ds(0, ds)], local_sem.at[2]),
            pltpu.make_async_copy(n_tea, near.at[:, pl.ds(ds, dt)], local_sem.at[3]),
        ]

    @pl.when(role == 0)
    def _():
        for c in loads(txt_stu, txt_tea, img_stu, img_tea):
            c.start()

    @pl.when(role == 1)
    def _():
        for c in loads(img_stu, img_tea, txt_stu, txt_tea):
            c.start()

    ids_load = pltpu.make_async_copy(ids, own_ids, local_sem.at[4])
    ids_load.start()

    barrier = pltpu.get_barrier_semaphore()
    for k in range(1, n_blk):
        pl.semaphore_signal(
            barrier, inc=1, device_id=at_blk(lax.rem(b + k, n_blk)), device_id_type=MESH
        )
    for k in range(1, n_grp):
        pl.semaphore_signal(
            barrier,
            inc=1,
            device_id={"blk": b, "grp": lax.rem(g + k, n_grp)},
            device_id_type=MESH,
        )
    for c in loads(txt_stu, txt_tea, img_stu, img_tea):
        c.wait()
    ids_load.wait()
    pl.semaphore_wait(barrier, n_blk - 1 + n_grp - 1)

    def remote(src, dst, send, recv, to):
        return pltpu.make_async_remote_copy(
            src_ref=src, dst_ref=dst, send_sem=send, recv_sem=recv,
            device_id=to, device_id_type=MESH,
        )

    fr = size // F_CHUNKS
    nr = size // N_CHUNKS
    ids_f = remote(own_ids, far_ids_in, ids_send.at[0], ids_recv.at[0], at_blk(far_to))
    ids_n = remote(own_ids, near_ids_in, ids_send.at[1], ids_recv.at[1], at_blk(near_to))
    ids_n.start()
    ids_f.start()
    near_copies = [
        remote(
            near.at[pl.ds(j * nr, nr)], near_in.at[pl.ds(j * nr, nr)],
            near_send.at[j], near_recv.at[j], at_blk(near_to),
        )
        for j in range(N_CHUNKS)
    ]
    far_copies = [
        remote(
            far.at[pl.ds(i * fr, fr)], far_in.at[pl.ds(i * fr, fr)],
            far_send.at[i], far_recv.at[i], at_blk(far_to),
        )
        for i in range(F_CHUNKS)
    ]
    for c in near_copies:
        c.start()
    for c in far_copies:
        c.start()

    scale_s = 2.0 / math.sqrt(ds)
    scale_t = 2.0 / math.sqrt(dt)

    def as_column(row):
        return jnp.transpose(jnp.broadcast_to(row, (128, row.shape[1])))[:, 0:1]

    def weigh(f, n, f_id, n_id):
        s = dot_nt(f[:, :ds], n[:, :ds]) * (0.5 * scale_s) - 0.5
        q = dot_nt(f[:, ds:], n[:, ds:]) * (0.5 * scale_t) - 0.5
        shift = jnp.where(f_id == n_id, -0.25, 0.25)
        return 0.5 * jnp.tanh(s) - 0.25 * jnp.tanh(q) + shift

    own_row = own_ids[...]
    own_col = as_column(own_row)

    w = weigh(far[...], near[...], own_col, own_row)
    total[...] = fold(w)
    wb = w.astype(jnp.bfloat16)
    acc_far[...] = dot_nn(wb, near[:, :ds])
    acc_near[...] = dot_tn(wb, far[:, :ds])

    ids_n.wait_recv()
    near_row = near_ids_in[...]
    for j in range(N_CHUNKS):
        near_copies[j].wait_recv()
        rows = pl.ds(j * nr, nr)
        w = weigh(near_in[rows, :], far[...], as_column(near_row)[j * nr : (j + 1) * nr], own_row)
        total[...] += fold(w)
        wb = w.astype(jnp.bfloat16)
        acc_far[...] += dot_tn(wb, near_in[rows, pl.ds(0, ds)])
        acc_pn[rows, :] = dot_nn(wb, far[:, :ds])

    def share_total():
        stage1_own[...] = total[...]
        stage1[pl.ds(b, 1)] = total[...][None]
        s1 = []
        for k in range(1, n_blk):
            c = remote(
                stage1_own, stage1.at[b], s1_send.at[k - 1], s1_recv.at[k - 1],
                at_blk(lax.rem(b + k, n_blk)),
            )
            c.start()
            s1.append(c)
        return s1

    ids_f.wait_recv()
    far_col = as_column(far_ids_in[...])
    pf_copies = []
    for i in range(F_CHUNKS):
        far_copies[i].wait_recv()
        rows = pl.ds(i * fr, fr)
        f = far_in[rows, :]
        f_id = far_col[i * fr : (i + 1) * fr]
        w1 = weigh(f, near[...], f_id, own_row)
        w2 = weigh(f, near_in[...], f_id, near_row)
        total[...] += fold(w1) + fold(w2)
        if i == F_CHUNKS - 1:
            s1 = share_total()
        w1 = w1.astype(jnp.bfloat16)
        w2 = w2.astype(jnp.bfloat16)
        back = dot_nn(w1, near[:, :ds]) + dot_nn(w2, near_in[:, :ds])
        pf_out[rows, :] = (back * scale_s).astype(jnp.bfloat16)
        c = remote(
            pf_out.at[rows], pf_in.at[rows], pf_send.at[i], pf_recv.at[i], at_blk(far_from)
        )
        c.start()
        pf_copies.append(c)
        acc_near[...] += dot_tn(w1, f[:, :ds])
        acc_pn[...] += dot_tn(w2, f[:, :ds])

    pr = size // OUT_CHUNKS
    pn_copies = []
    for j in range(OUT_CHUNKS):
        rows = pl.ds(j * pr, pr)
        pn_out[rows, :] = (acc_pn[rows, :] * scale_s).astype(jnp.bfloat16)
        c = remote(
            pn_out.at[rows], pn_in.at[rows], pn_send.at[j], pn_recv.at[j], at_blk(near_from)
        )
        c.start()
        pn_copies.append(c)

    for c in s1:
        c.wait_recv()
    part = stage1[0]
    for k in range(1, n_blk):
        part = part + stage1[k]
    stage2_own[...] = part
    stage2[pl.ds(g, 1)] = part[None]
    s2 = []
    for k in range(1, n_grp):
        c = remote(
            stage2_own, stage2.at[g], s2_send.at[k - 1], s2_recv.at[k - 1],
            {"blk": b, "grp": lax.rem(g + k, n_grp)},
        )
        c.start()
        s2.append(c)

    written = []

    def finish(copies, acc, arrived, rows_each, out_a, out_b, first):
        for i, c in enumerate(copies):
            c.wait_recv()
            rows = pl.ds(i * rows_each, rows_each)
            acc[rows, :] = acc[rows, :] * scale_s + arrived[rows, :].astype(jnp.float32)
            put_a = pltpu.make_async_copy(acc.at[rows], out_a.at[rows], out_sem.at[first + i])
            put_b = pltpu.make_async_copy(acc.at[rows], out_b.at[rows], out_sem.at[first + i])
            written.append(put_a)

            @pl.when(role == 0)
            def _():
                put_a.start()

            @pl.when(role == 1)
            def _():
                put_b.start()

    finish(pf_copies, acc_far, pf_in, fr, out_txt, out_img, 0)
    finish(pn_copies, acc_near, pn_in, pr, out_img, out_txt, F_CHUNKS)

    for c in s2:
        c.wait_recv()
    whole = stage2[0]
    for k in range(1, n_grp):
        whole = whole + stage2[k]
    out_bias[0, 0] = jnp.sum(whole) * inv_count

    for c in written:
        c.wait()
    for c in [ids_f, ids_n] + near_copies + far_copies + pf_copies + pn_copies + s1 + s2:
        c.wait_send()


def land(a, b, out_a, out_b, held, came, went):
    each = a.shape[0] // OUT_CHUNKS
    pieces = [(at, i) for i in range(OUT_CHUNKS) for at in range(2)]
    arrays = ((a, out_a), (b, out_b))
    ins, outs = [], []
    for at, i in pieces:
        rows = pl.ds(i * each, each)
        src, dst = arrays[at]
        ins.append(pltpu.make_async_copy(src.at[rows], held.at[at, rows], came.at[at, i]))
        outs.append(pltpu.make_async_copy(held.at[at, rows], dst.at[rows], went.at[at, i]))
    for c in ins:
        c.start()
    for c, d in zip(ins, outs):
        c.wait()
        d.start()
    for d in outs:
        d.wait()


def solution(mesh):
    n_blk, n_grp = mesh.shape["blk"], mesh.shape["grp"]

    def body(image_student, image_teacher, text_student, text_teacher, pair_ids):
        size, ds = image_student.shape[2:]
        dt = image_teacher.shape[3]
        bf, f32 = jnp.bfloat16, jnp.float32
        dma = lambda k: pltpu.SemaphoreType.DMA((max(k, 1),))
        count = float(n_blk * n_grp * WINDOW * size * size)
        img, txt, bias = pl.pallas_call(
            functools.partial(kernel, n_blk, n_grp, ds, 1.0 / count),
            out_shape=(
                jax.ShapeDtypeStruct((size, ds), f32),
                jax.ShapeDtypeStruct((size, ds), f32),
                jax.ShapeDtypeStruct((1, 1), f32),
            ),
            in_specs=[pl.BlockSpec(memory_space=pl.ANY)] * 5,
            out_specs=(
                pl.BlockSpec(memory_space=pl.ANY),
                pl.BlockSpec(memory_space=pl.ANY),
                pl.BlockSpec(memory_space=pltpu.SMEM),
            ),
            scratch_shapes=[
                pltpu.VMEM((size, ds + dt), bf),
                pltpu.VMEM((size, ds + dt), bf),
                pltpu.VMEM((1, size), jnp.int32),
                pltpu.VMEM((size, ds + dt), bf),
                pltpu.VMEM((size, ds + dt), bf),
                pltpu.VMEM((1, size), jnp.int32),
                pltpu.VMEM((1, size), jnp.int32),
                pltpu.VMEM((size, ds), f32),
                pltpu.VMEM((size, ds), f32),
                pltpu.VMEM((size, ds), f32),
                pltpu.VMEM((size, ds), bf),
                pltpu.VMEM((size, ds), bf),
                pltpu.VMEM((size, ds), bf),
                pltpu.VMEM((size, ds), bf),
                pltpu.VMEM((8, 128), f32),
                pltpu.VMEM((8, 128), f32),
                pltpu.VMEM((n_blk, 8, 128), f32),
                pltpu.VMEM((8, 128), f32),
                pltpu.VMEM((n_grp, 8, 128), f32),
                dma(5),
                dma(F_CHUNKS),
                dma(F_CHUNKS),
                dma(N_CHUNKS),
                dma(N_CHUNKS),
                dma(2),
                dma(2),
                dma(F_CHUNKS),
                dma(F_CHUNKS),
                dma(OUT_CHUNKS),
                dma(OUT_CHUNKS),
                dma(n_blk - 1),
                dma(n_blk - 1),
                dma(n_grp - 1),
                dma(n_grp - 1),
                dma(F_CHUNKS + OUT_CHUNKS),
            ],
            compiler_params=pltpu.CompilerParams(
                collective_id=0, has_side_effects=True, vmem_limit_bytes=62 * 1024 * 1024
            ),
        )(
            image_student[0, 0],
            image_teacher[0, 0],
            text_student[0, 0],
            text_teacher[0, 0],
            pair_ids[0],
        )
        img, txt = pl.pallas_call(
            land,
            out_shape=(
                jax.ShapeDtypeStruct((size, ds), f32),
                jax.ShapeDtypeStruct((size, ds), f32),
            ),
            in_specs=[pl.BlockSpec(memory_space=pl.ANY)] * 2,
            out_specs=[pl.BlockSpec(memory_space=pl.ANY)] * 2,
            scratch_shapes=[
                pltpu.VMEM((2, size, ds), f32),
                pltpu.SemaphoreType.DMA((2, OUT_CHUNKS)),
                pltpu.SemaphoreType.DMA((2, OUT_CHUNKS)),
            ],
            compiler_params=pltpu.CompilerParams(vmem_limit_bytes=62 * 1024 * 1024),
        )(img, txt)
        return img[None, None], txt[None, None], bias[0, 0]

    return jax.shard_map(
        body,
        mesh=mesh,
        in_specs=(
            P("blk", "grp", None, None),
            P("blk", "grp", None, None),
            P("blk", "grp", None, None),
            P("blk", "grp", None, None),
            P("blk", "grp", None),
        ),
        out_specs=(P("blk", "grp", None, None), P("blk", "grp", None, None), P()),
        check_vma=False,
    )
```
